32 devices in a mesh: gx: 4 (over x, core), gy: 2 (over y), gz: 4 (over z).
Axes of the slice: x: 2, y: 2, z: 4, core: 2. Of those that a mesh axis runs over, the one named last changes fastest.
Arguments:
- solution: float32 [16, 8, 16, 256], P(None, 'gx', 'gz', 'gy'), may hold values from -0.6 to 0.6
- residual: float32 [16, 8, 16, 256], P(None, 'gx', 'gz', 'gy'), may hold values from -6 to 6
- direction_prev: float32 [16, 8, 16, 256], P(None, 'gx', 'gz', 'gy'), may hold values from -0.3 to 0.3, as said below
- image_prev: float32 [16, 8, 16, 256], P(None, 'gx', 'gz', 'gy'), may hold values from -9 to 9, as said below
- gram_prev: float32 [16, 16], replicated, may hold values from -32768 to 32768, as said below
Outputs:
- solution_new: float32 [16, 8, 16, 256], P(None, 'gx', 'gz', 'gy')
- residual_new: float32 [16, 8, 16, 256], P(None, 'gx', 'gz', 'gy')
- direction: float32 [16, 8, 16, 256], P(None, 'gx', 'gz', 'gy')
The draws below stay inside these ranges and needn't reach their ends.
Inputs may be any that keep to these rules, and one draw needn't show every extreme that they name: direction_prev is a field of order 0.05. image_prev equals A direction_prev, computed in float32. gram_prev is symmetric and positive definite.
All inputs are finite; a program needn't handle non-finite values.
Results may differ from the reference program's by a relative error of at most 0.0001.
Values sent between devices are 32-bit elements; how exact they have to be, the bound alone decides.
No kernel may reach another device: no remote copies, remote signals or barrier semaphores. Data moves between devices by JAX's collectives and lax.ppermute only.
A program may use at most 64 MiB of HBM per device.

```python
import jax
import jax.numpy as jnp
from jax import lax

RHS = 16
NX = 8
NZ = 16
NY = 256


def box_total(padded):
    total = padded[:, :-2] + padded[:, 1:-1] + padded[:, 2:]
    total = total[:, :, :-2] + total[:, :, 1:-1] + total[:, :, 2:]
    return total[:, :, :, :-2] + total[:, :, :, 1:-1] + total[:, :, :, 2:]


def shared_fields(key):
    base = jax.random.fold_in(key, 11)
    shape = (RHS, NX, NZ, NY)
    field = jnp.clip(0.04 * jax.random.normal(base, shape, jnp.float32), -0.24, 0.24)
    padded = jnp.pad(field, ((0, 0), (1, 1), (1, 1), (1, 1)))
    image = 27.0 * field - box_total(padded)
    return (field, image)


def draw_direction_prev(key, part):
    return shared_fields(key)[0]


def draw_image_prev(key, part):
    return shared_fields(key)[1]


def draw_gram_prev(key, part):
    base = jax.random.fold_in(key, 23)
    noise = jax.random.normal(base, (RHS, RHS), jnp.float32)
    matrix = jnp.eye(RHS, dtype=jnp.float32) + 0.05 * (noise + noise.T)
    return matrix * (NX * NY * NZ / 20.0)


def block_scale(key, extent, cuts, smallest, high):
    factor_of, own = 1.0, jax.random.fold_in(key, 6)
    for dim, parts in cuts:
        steps = jnp.exp(jax.random.uniform(jax.random.fold_in(own, dim), (parts,), jnp.float32, smallest / len(cuts), high / len(cuts)))
        factor_of = factor_of * jnp.repeat(steps, extent[dim] // parts).reshape([-1 if axis == dim else 1 for axis in range(len(extent))])
    return factor_of


def gaussian(key, extent, scale, limit, shards=(), kind=jnp.bfloat16):
    level = block_scale(key, extent, shards, -0.22, 0.18) if shards else 1.0
    drawn = jax.random.normal(key, extent, jnp.float32) * scale * level
    return jnp.minimum(jnp.maximum(drawn, -limit), limit).astype(kind)


def setup_inputs(seed: int = 0) -> dict:
    key_of = jax.random.split(jax.random.key(seed), 6)
    return {
        "solution": gaussian(key_of[0], (RHS, NX, NZ, NY), 0.1, 0.6, ((1, 4), (2, 4), (3, 2)), jnp.float32),
        "residual": gaussian(key_of[1], (RHS, NX, NZ, NY), 1.0, 6.0, ((1, 4), (2, 4), (3, 2)), jnp.float32),
        "direction_prev": draw_direction_prev(jax.random.fold_in(key_of[5], 71), 0),
        "image_prev": draw_image_prev(jax.random.fold_in(key_of[5], 71), 0),
        "gram_prev": draw_gram_prev(jax.random.fold_in(key_of[5], 71), 0),
    }


def pad_field(field):
    return jnp.pad(field, ((0, 0), (1, 1), (1, 1), (1, 1)))

def box_sum(padded):
    total = padded[:, :-2] + padded[:, 1:-1] + padded[:, 2:]
    total = total[:, :, :-2] + total[:, :, 1:-1] + total[:, :, 2:]
    return total[:, :, :, :-2] + total[:, :, :, 1:-1] + total[:, :, :, 2:]

def colors_of(shape):
    first = lax.broadcasted_iota(jnp.int32, shape, 1) % 2
    second = lax.broadcasted_iota(jnp.int32, shape, 2) % 2
    third = lax.broadcasted_iota(jnp.int32, shape, 3) % 2
    return 4 * first + 2 * second + third

def gram(left, right):
    return jnp.einsum('kxzy,lxzy->kl', left, right, precision=lax.Precision.HIGHEST)

def combine(field, mixing):
    return jnp.einsum('kxzy,kl->lxzy', field, mixing, precision=lax.Precision.HIGHEST)

def spd_solve(matrix, target):
    order = matrix.shape[0]
    sym = 0.5 * (matrix + matrix.T)
    lower = jnp.zeros_like(sym)
    for col in range(order):
        column = sym[col:, col] - lax.optimization_barrier(jnp.sum(lower[col:, :col] * lower[col, :col][None, :], axis=1))
        pivot = jnp.sqrt(column[0])
        lower = lower.at[col:, col].set(column / pivot)
    middle = jnp.zeros_like(target)
    for row in range(order):
        value = target[row] - lax.optimization_barrier(jnp.sum(lower[row, :row][:, None] * middle[:row], axis=0))
        middle = middle.at[row].set(value / lower[row, row])
    answer = jnp.zeros_like(target)
    for row in range(order - 1, -1, -1):
        value = middle[row] - lax.optimization_barrier(jnp.sum(lower[row + 1:, row][:, None] * answer[row + 1:], axis=0))
        answer = answer.at[row].set(value / lower[row, row])
    return answer

def reference(solution, residual, direction_prev, image_prev, gram_prev):
    colors = colors_of(residual.shape)
    smoothed = jnp.where(colors == 0, residual / 26.0, jnp.float32(0.0))
    for shade in list(range(1, 8)) + list(range(6, -1, -1)):
        boxed = box_sum(pad_field(smoothed))
        smoothed = jnp.where(colors == shade, (residual + boxed - smoothed) / 26.0, smoothed)
    image = 27.0 * smoothed - box_sum(pad_field(smoothed))
    gram_zr = gram(smoothed, residual)
    beta_mix = spd_solve(gram_prev, gram_zr)
    direction = smoothed + combine(direction_prev, beta_mix)
    image_new = image + combine(image_prev, beta_mix)
    curvature = gram(direction, image_new)
    alpha_step = spd_solve(curvature, gram_zr)
    solution_new = solution + combine(direction, alpha_step)
    residual_new = residual - combine(image_new, alpha_step)
    return (solution_new, residual_new, direction)
```

```python
import functools

import jax
import jax.numpy as jnp
from jax import lax
from jax.experimental import pallas as pl
from jax.experimental.pallas import tpu as pltpu
from jax.sharding import PartitionSpec as P

HIGHEST = lax.Precision.HIGHEST
REACH = {"gx": (2, 3), "gz": (6, 7), "gy": (14, 15)}
HALO = 16


def shifted(value, axis, step):
    devices = lax.axis_size(axis)
    pairs = [(i, i - step) for i in range(devices) if 0 <= i - step < devices]
    return lax.ppermute(value, axis, pairs)


def block_reach(axis, length):
    low, high = REACH[axis]
    return (-(-low // length), -(-high // length))


def gathered(axis, length):
    low, high = block_reach(axis, length)
    return lax.axis_size(axis) <= low + high + 1


def neighbours(value, axis, length):
    if gathered(axis, length):
        return lax.all_gather(value, axis)
    low, high = block_reach(axis, length)
    return jnp.stack([value if s == 0 else shifted(value, axis, s) for s in range(-low, high + 1)])


def beside(value):
    devices, width = (lax.axis_size("gy"), HALO)
    first, last = value[..., :width], value[..., -width:]
    if devices == 2:
        both = lax.ppermute(jnp.concatenate([first, last], axis=-1), "gy", [(0, 1), (1, 0)])
    else:
        both = jnp.concatenate([shifted(first, "gy", 1), shifted(last, "gy", -1)], axis=-1)
    rows, rhs, lanes = value.shape
    group = lanes // (2 * width)
    both = both.reshape(rows // group, group, rhs, 2, width).transpose(0, 2, 3, 1, 4)
    return both.reshape(rows // group, rhs, lanes)


def smooth_kernel(where, upper, lower, prev, image_prev, smoothed_out, image_out, gram_out, x00, x01, x10, x11, *, dims, counts, full):
    lx, lz, rows, lanes = dims
    nx, nz, ny = counts
    at_x, at_z, at_y = where[0], where[1], where[2]
    total = 2 * lanes
    lane = lax.broadcasted_iota(jnp.int32, (1, total), 1)
    half = lanes // 2
    group = half // HALO
    inside = jnp.ones((1, total), jnp.float32)
    inside = jnp.where((lane >= lanes) & (lane < lanes + half) & (at_y == ny - 1), 0.0, inside)
    inside = jnp.where((lane >= lanes + half) & (at_y == 0), 0.0, inside)
    inside = inside * (1.0 / 26.0)
    even_lanes = jnp.where(lane % 2 == 0, inside, 0.0)
    odd_lanes = jnp.where(lane % 2 == 1, inside, 0.0)
    low_x, low_z = block_low("gx", lx), block_low("gz", lz)

    def source(li, lj):
        gi, gj = at_x * lx + li, at_z * lz + lj
        valid = (gi >= 0) & (gi < nx * lx) & (gj >= 0) & (gj < nz * lz)
        gi, gj = jnp.clip(gi, 0, nx * lx - 1), jnp.clip(gj, 0, nz * lz - 1)
        bx, bz = gi // lx, gj // lz
        sub = (gi - bx * lx) * lz + gj - bz * lz
        bx = bx if full[0] else bx - at_x + low_x
        bz = bz if full[1] else bz - at_z + low_z
        scale = jnp.where(valid, 1.0, 0.0).astype(jnp.float32)
        place = (lj % lz) % group
        main = jnp.concatenate([upper[bx, bz, sub], lower[bx, bz, sub]], axis=0)
        packed = rows + sub // group
        tile = jnp.concatenate([upper[bx, bz, packed], lower[bx, bz, packed]], axis=0)
        after = pltpu.roll(tile, (lanes - HALO * place) % lanes, 1)
        before = pltpu.roll(tile, (half - HALO * (place + 1)) % lanes, 1)
        side = jnp.where(lane[:, :lanes] < half, after, before)
        return jnp.concatenate([main, side], axis=1), even_lanes * scale, odd_lanes * scale

    def pair(x):
        return pltpu.roll(x, 1, 1) + pltpu.roll(x, total - 1, 1)

    def box(x):
        return x + pair(x)

    ex, ez = lx // 2 + 3, (lz + 14) // 2

    def sides_j0(ref, a, b):
        return ref[a, b - 1] + ref[a, b]

    def sides_j1(ref, a, b):
        return ref[a, b] + ref[a, b + 1]

    def loop(count, start, step):
        def run(a, carry):
            step(a)
            return carry

        lax.fori_loop(start, start + count, run, 0)

    def f0e(a):
        for b in range(ez):
            r, se, so = source(-2 + 2 * a, -6 + 2 * b)
            xe = r * se
            x00[a, b] = xe + (r + pair(xe)) * so

    def f0o(a):
        for b in range(ez - 1):
            r, se, so = source(-2 + 2 * a, -5 + 2 * b)
            q = r + box(sides_j1(x00, a, b))
            xe = q * se
            x01[a, b] = xe + (q + pair(xe)) * so

    def f1e(a):
        for b in range(1, ez - 1):
            r, se, so = source(-1 + 2 * a, -6 + 2 * b)
            near = x00[a, b] + x00[a + 1, b] + sides_j0(x01, a, b) + sides_j0(x01, a + 1, b)
            q = r + box(near)
            xe = q * se
            x10[a, b] = xe + (q + pair(xe)) * so

    def f1o(a):
        for b in range(1, ez - 2):
            r, se, so = source(-1 + 2 * a, -5 + 2 * b)
            near = x01[a, b] + x01[a + 1, b] + sides_j1(x00, a, b) + sides_j1(x00, a + 1, b) + sides_j1(x10, a, b)
            q = r + box(near)
            xo = (q + pair(q * se)) * so
            x11[a, b] = (q + pair(xo)) * se + xo

    def b1e(a):
        for b in range(2, ez - 2):
            r, se, so = source(-1 + 2 * a, -6 + 2 * b)
            near = x00[a, b] + x00[a + 1, b] + sides_j0(x01, a, b) + sides_j0(x01, a + 1, b) + sides_j0(x11, a, b)
            q = r + box(near)
            xo = (q + pair(x10[a, b])) * so
            x10[a, b] = (q + pair(xo)) * se + xo

    def b0o(a):
        for b in range(2, ez - 3):
            r, se, so = source(-2 + 2 * a, -5 + 2 * b)
            near = x11[a - 1, b] + x11[a, b] + sides_j1(x10, a - 1, b) + sides_j1(x10, a, b) + sides_j1(x00, a, b)
            q = r + box(near)
            xo = (q + pair(x01[a, b])) * so
            x01[a, b] = (q + pair(xo)) * se + xo

    def b0e(a):
        for b in range(3, ez - 3):
            r, se, so = source(-2 + 2 * a, -6 + 2 * b)
            near = x10[a - 1, b] + x10[a, b] + sides_j0(x11, a - 1, b) + sides_j0(x11, a, b) + sides_j0(x01, a, b)
            q = r + box(near)
            xo = (q + pair(x00[a, b])) * so
            x00[a, b] = (q + pair(xo)) * se + xo

    loop(ex, 0, f0e)
    loop(ex, 0, f0o)
    loop(ex - 1, 0, f1e)
    loop(ex - 1, 0, f1o)
    loop(ex - 1, 0, b1e)
    loop(ex - 2, 1, b0o)
    loop(ex - 2, 1, b0e)

    def cell(i, j):
        a = (i + 2) // 2 if i % 2 == 0 else (i + 1) // 2
        b = (j + 6) // 2 if j % 2 == 0 else (j + 5) // 2
        return ((x00, x01), (x10, x11))[i % 2][j % 2][a, b]

    own = []
    for i in range(lx):
        for j in range(lz):
            near = functools.reduce(jnp.add, [cell(i + u, j + v) for u in (-1, 0, 1) for v in (-1, 0, 1)])
            mine = cell(i, j)
            image = 27.0 * mine - box(near)
            at = (i * lz + j) * lanes
            smoothed_out[:, at : at + lanes] = mine[:, :lanes]
            image_out[:, at : at + lanes] = image[:, :lanes]
            own.append(source(i, j)[0][:, :lanes])
    left = jnp.concatenate([smoothed_out[...], prev[...]], axis=0)
    right = jnp.concatenate([jnp.concatenate(own, axis=1), image_out[...], image_prev[...]], axis=0)
    gram_out[...] = lax.dot_general(left, right, (((1,), (1,)), ((), ())), precision=HIGHEST)


def block_low(axis, length):
    return -(-REACH[axis][0] // length)


def spd_solve(matrix, target):
    order = matrix.shape[0]
    sym = 0.5 * (matrix + matrix.T)
    work = jnp.concatenate([sym, target], axis=1)
    row = lax.broadcasted_iota(jnp.int32, (order, 1), 0)
    for k in range(order):
        scaled = work[k : k + 1] / work[k : k + 1, k : k + 1]
        factor = work[:, k : k + 1]
        work = jnp.where(row == k, scaled, work - factor * scaled)
    return work[:, order:]


def dot(left, right):
    return jnp.dot(left, right, precision=HIGHEST)


def finish_kernel(grams, gram_prev, solution, residual, prev, image_prev, smoothed, image, solution_out, residual_out, direction_out):
    n = gram_prev.shape[0]
    total = jnp.sum(grams[...], axis=0)
    gram_zr, gram_zw, gram_zq = total[:n, :n], total[:n, n : 2 * n], total[:n, 2 * n :]
    gram_pw, gram_pq = total[n:, n : 2 * n], total[n:, 2 * n :]
    beta = spd_solve(gram_prev[...], gram_zr)
    turned = beta.T
    curvature = gram_zw + dot(gram_zq, beta) + dot(turned, gram_pw + dot(gram_pq, beta))
    direction = smoothed[...] + dot(turned, prev[...])
    image_new = image[...] + dot(turned, image_prev[...])
    alpha = spd_solve(curvature, gram_zr).T
    direction_out[...] = direction
    solution_out[...] = solution[...] + dot(alpha, direction)
    residual_out[...] = residual[...] - dot(alpha, image_new)


def gather_grams(gram):
    for axis in ("gx", "gy", "gz"):
        others = [lax.ppermute(gram, axis, [(i, (i + k) % lax.axis_size(axis)) for i in range(lax.axis_size(axis))])
                  for k in range(1, lax.axis_size(axis))]
        gram = functools.reduce(jnp.add, others, gram)
    return gram[None]


def body(solution, residual, direction_prev, image_prev, gram_prev):
    rhs, lx, lz, lanes = residual.shape
    rows = lx * lz
    counts = tuple(lax.axis_size(axis) for axis in ("gx", "gz", "gy"))
    where = jnp.stack([lax.axis_index(axis) for axis in ("gx", "gz", "gy")]).astype(jnp.int32)
    flat = [v.reshape(rhs, rows * lanes) for v in (solution, residual, direction_prev, image_prev)]
    turned = residual.transpose(1, 2, 0, 3).reshape(rows, rhs, lanes)
    wide = jnp.concatenate([turned, beside(turned)], axis=0)
    wide = neighbours(wide, "gz", lz)
    upper = neighbours(wide[:, :, : rhs // 2], "gx", lx)
    lower = neighbours(wide[:, :, rhs // 2 :], "gx", lx)
    full = (gathered("gx", lx), gathered("gz", lz))
    ex, ez = lx // 2 + 3, (lz + 14) // 2
    out = jax.ShapeDtypeStruct((rhs, rows * lanes), jnp.float32)
    vmem = pl.BlockSpec(memory_space=pltpu.VMEM)
    smoothed, image, gram = pl.pallas_call(
        functools.partial(smooth_kernel, dims=(lx, lz, rows, lanes), counts=counts, full=full),
        out_shape=(out, out, jax.ShapeDtypeStruct((2 * rhs, 3 * rhs), jnp.float32)),
        in_specs=[pl.BlockSpec(memory_space=pltpu.SMEM)] + [vmem] * 4,
        out_specs=(vmem, vmem, vmem),
        scratch_shapes=[pltpu.VMEM((ex, ez, rhs, 2 * lanes), jnp.float32) for _ in range(4)],
        name="smooth",
    )(where, upper, lower, flat[2], flat[3])
    grams = gather_grams(gram)
    outs = pl.pallas_call(
        finish_kernel,
        out_shape=(out, out, out),
        in_specs=[vmem] * 8,
        out_specs=(vmem,) * 3,
        name="finish",
    )(grams, gram_prev, *flat, smoothed, image)
    return tuple(v.reshape(residual.shape) for v in outs)


def solution(mesh):
    field = P(None, "gx", "gz", "gy")
    return jax.shard_map(
        body, mesh=mesh, in_specs=(field,) * 4 + (P(),), out_specs=(field,) * 3, check_vma=False
    )
```

```python
import functools

import jax
import jax.numpy as jnp
from jax import lax
from jax.experimental import pallas as pl
from jax.experimental.pallas import tpu as pltpu
from jax.sharding import PartitionSpec as P

HIGHEST = lax.Precision.HIGHEST
REACH = {"gx": (2, 3), "gz": (6, 7), "gy": (14, 15)}
HALO = 16


def shifted(value, axis, step):
    devices = lax.axis_size(axis)
    pairs = [(i, i - step) for i in range(devices) if 0 <= i - step < devices]
    return lax.ppermute(value, axis, pairs)


def block_reach(axis, length):
    low, high = REACH[axis]
    return (-(-low // length), -(-high // length))


def gathered(axis, length):
    low, high = block_reach(axis, length)
    return lax.axis_size(axis) <= low + high + 1


def neighbours(value, axis, length):
    if gathered(axis, length):
        return lax.all_gather(value, axis)
    low, high = block_reach(axis, length)
    return jnp.stack([value if s == 0 else shifted(value, axis, s) for s in range(-low, high + 1)])


def beside(value):
    devices, width = (lax.axis_size("gy"), HALO)
    first, last = value[..., :width], value[..., -width:]
    if devices == 2:
        both = lax.ppermute(jnp.concatenate([first, last], axis=-1), "gy", [(0, 1), (1, 0)])
    else:
        both = jnp.concatenate([shifted(first, "gy", 1), shifted(last, "gy", -1)], axis=-1)
    rows, rhs, lanes = value.shape
    group = lanes // (2 * width)
    both = both.reshape(rows // group, group, rhs, 2, width).transpose(0, 2, 3, 1, 4)
    return both.reshape(rows // group, rhs, lanes)


def smooth_kernel(where, upper, lower, prev, image_prev, smoothed_out, image_out, gram_out, x00, x01, x10, x11, *, dims, counts, full):
    lx, lz, rows, lanes = dims
    nx, nz, ny = counts
    at_x, at_z, at_y = where[0], where[1], where[2]
    total = 2 * lanes
    lane = lax.broadcasted_iota(jnp.int32, (1, total), 1)
    half = lanes // 2
    group = half // HALO
    inside = jnp.ones((1, total), jnp.float32)
    inside = jnp.where((lane >= lanes) & (lane < lanes + half) & (at_y == ny - 1), 0.0, inside)
    inside = jnp.where((lane >= lanes + half) & (at_y == 0), 0.0, inside)
    inside = inside * (1.0 / 26.0)
    even_lanes = jnp.where(lane % 2 == 0, inside, 0.0)
    odd_lanes = jnp.where(lane % 2 == 1, inside, 0.0)
    low_x, low_z = block_low("gx", lx), block_low("gz", lz)

    def source(li, lj):
        gi, gj = at_x * lx + li, at_z * lz + lj
        valid = (gi >= 0) & (gi < nx * lx) & (gj >= 0) & (gj < nz * lz)
        gi, gj = jnp.clip(gi, 0, nx * lx - 1), jnp.clip(gj, 0, nz * lz - 1)
        bx, bz = gi // lx, gj // lz
        sub = (gi - bx * lx) * lz + gj - bz * lz
        bx = bx if full[0] else bx - at_x + low_x
        bz = bz if full[1] else bz - at_z + low_z
        scale = jnp.where(valid, 1.0, 0.0).astype(jnp.float32)
        place = (lj % lz) % group
        main = jnp.concatenate([upper[bx, bz, sub], lower[bx, bz, sub]], axis=0)
        packed = rows + sub // group
        tile = jnp.concatenate([upper[bx, bz, packed], lower[bx, bz, packed]], axis=0)
        after = pltpu.roll(tile, (lanes - HALO * place) % lanes, 1)
        before = pltpu.roll(tile, (half - HALO * (place + 1)) % lanes, 1)
        side = jnp.where(lane[:, :lanes] < half, after, before)
        return jnp.concatenate([main, side], axis=1), even_lanes * scale, odd_lanes * scale

    def pair(x):
        return pltpu.roll(x, 1, 1) + pltpu.roll(x, total - 1, 1)

    def box(x):
        return x + pair(x)

    ex, ez = lx // 2 + 3, (lz + 14) // 2

    def sides_j0(ref, a, b):
        return ref[a, b - 1] + ref[a, b]

    def sides_j1(ref, a, b):
        return ref[a, b] + ref[a, b + 1]

    def loop(count, start, step):
        def run(a, carry):
            step(a)
            return carry

        lax.fori_loop(start, start + count, run, 0)

    def f0e(a):
        for b in range(ez):
            r, se, so = source(-2 + 2 * a, -6 + 2 * b)
            xe = r * se
            x00[a, b] = xe + (r + pair(xe)) * so

    def f0o(a):
        for b in range(ez - 1):
            r, se, so = source(-2 + 2 * a, -5 + 2 * b)
            q = r + box(sides_j1(x00, a, b))
            xe = q * se
            x01[a, b] = xe + (q + pair(xe)) * so

    def f1e(a):
        for b in range(1, ez - 1):
            r, se, so = source(-1 + 2 * a, -6 + 2 * b)
            near = x00[a, b] + x00[a + 1, b] + sides_j0(x01, a, b) + sides_j0(x01, a + 1, b)
            q = r + box(near)
            xe = q * se
            x10[a, b] = xe + (q + pair(xe)) * so

    def f1o(a):
        for b in range(1, ez - 2):
            r, se, so = source(-1 + 2 * a, -5 + 2 * b)
            near = x01[a, b] + x01[a + 1, b] + sides_j1(x00, a, b) + sides_j1(x00, a + 1, b) + sides_j1(x10, a, b)
            q = r + box(near)
            xo = (q + pair(q * se)) * so
            x11[a, b] = (q + pair(xo)) * se + xo

    def b1e(a):
        for b in range(2, ez - 2):
            r, se, so = source(-1 + 2 * a, -6 + 2 * b)
            near = x00[a, b] + x00[a + 1, b] + sides_j0(x01, a, b) + sides_j0(x01, a + 1, b) + sides_j0(x11, a, b)
            q = r + box(near)
            xo = (q + pair(x10[a, b])) * so
            x10[a, b] = (q + pair(xo)) * se + xo

    def b0o(a):
        for b in range(2, ez - 3):
            r, se, so = source(-2 + 2 * a, -5 + 2 * b)
            near = x11[a - 1, b] + x11[a, b] + sides_j1(x10, a - 1, b) + sides_j1(x10, a, b) + sides_j1(x00, a, b)
            q = r + box(near)
            xo = (q + pair(x01[a, b])) * so
            x01[a, b] = (q + pair(xo)) * se + xo

    def b0e(a):
        for b in range(3, ez - 3):
            r, se, so = source(-2 + 2 * a, -6 + 2 * b)
            near = x10[a - 1, b] + x10[a, b] + sides_j0(x11, a - 1, b) + sides_j0(x11, a, b) + sides_j0(x01, a, b)
            q = r + box(near)
            xo = (q + pair(x00[a, b])) * so
            x00[a, b] = (q + pair(xo)) * se + xo

    loop(ex, 0, f0e)
    loop(ex, 0, f0o)
    loop(ex - 1, 0, f1e)
    loop(ex - 1, 0, f1o)
    loop(ex - 1, 0, b1e)
    loop(ex - 2, 1, b0o)
    loop(ex - 2, 1, b0e)

    def cell(i, j):
        a = (i + 2) // 2 if i % 2 == 0 else (i + 1) // 2
        b = (j + 6) // 2 if j % 2 == 0 else (j + 5) // 2
        return ((x00, x01), (x10, x11))[i % 2][j % 2][a, b]

    own = []
    for i in range(lx):
        for j in range(lz):
            near = functools.reduce(jnp.add, [cell(i + u, j + v) for u in (-1, 0, 1) for v in (-1, 0, 1)])
            mine = cell(i, j)
            image = 27.0 * mine - box(near)
            at = (i * lz + j) * lanes
            smoothed_out[:, at : at + lanes] = mine[:, :lanes]
            image_out[:, at : at + lanes] = image[:, :lanes]
            own.append(source(i, j)[0][:, :lanes])
    left = jnp.concatenate([smoothed_out[...], prev[...]], axis=0)
    right = jnp.concatenate([jnp.concatenate(own, axis=1), image_out[...], image_prev[...]], axis=0)
    gram_out[...] = lax.dot_general(left, right, (((1,), (1,)), ((), ())), precision=HIGHEST)


def block_low(axis, length):
    return -(-REACH[axis][0] // length)


def spd_solve(matrix, target):
    order = matrix.shape[0]
    sym = 0.5 * (matrix + matrix.T)
    work = jnp.concatenate([sym, target], axis=1)
    row = lax.broadcasted_iota(jnp.int32, (order, 1), 0)
    for k in range(order):
        scaled = work[k : k + 1] / work[k : k + 1, k : k + 1]
        factor = work[:, k : k + 1]
        work = jnp.where(row == k, scaled, work - factor * scaled)
    return work[:, order:]


def dot(left, right):
    return jnp.dot(left, right, precision=HIGHEST)


def invert_kernel(matrix, out):
    order = matrix.shape[0]
    row = lax.broadcasted_iota(jnp.int32, (order, order), 0)
    col = lax.broadcasted_iota(jnp.int32, (order, order), 1)
    out[...] = spd_solve(matrix[...], jnp.where(row == col, 1.0, 0.0).astype(jnp.float32))


def finish_kernel(grams, inverse, solution, residual, prev, image_prev, smoothed, image, solution_out, residual_out, direction_out):
    n = inverse.shape[0]
    total = jnp.sum(grams[...], axis=0)
    gram_zr, gram_zw, gram_zq = total[:n, :n], total[:n, n : 2 * n], total[:n, 2 * n :]
    gram_pw, gram_pq = total[n:, n : 2 * n], total[n:, 2 * n :]
    beta = dot(inverse[...], gram_zr)
    turned = beta.T
    curvature = gram_zw + dot(gram_zq, beta) + dot(turned, gram_pw + dot(gram_pq, beta))
    direction = smoothed[...] + dot(turned, prev[...])
    image_new = image[...] + dot(turned, image_prev[...])
    alpha = spd_solve(curvature, gram_zr).T
    values = (direction, solution[...] + dot(alpha, direction), residual[...] - dot(alpha, image_new))
    _, lx, lz, lanes = direction_out.shape
    for value, out in zip(values, (direction_out, solution_out, residual_out)):
        for i in range(lx):
            for j in range(lz):
                at = (i * lz + j) * lanes
                out[:, i, j, :] = value[:, at : at + lanes]


def gather_grams(gram):
    for axis in ("gx", "gy", "gz"):
        others = [lax.ppermute(gram, axis, [(i, (i + k) % lax.axis_size(axis)) for i in range(lax.axis_size(axis))])
                  for k in range(1, lax.axis_size(axis))]
        gram = functools.reduce(jnp.add, others, gram)
    return gram[None]


def body(solution, residual, direction_prev, image_prev, gram_prev):
    rhs, lx, lz, lanes = residual.shape
    rows = lx * lz
    counts = tuple(lax.axis_size(axis) for axis in ("gx", "gz", "gy"))
    where = jnp.stack([lax.axis_index(axis) for axis in ("gx", "gz", "gy")]).astype(jnp.int32)
    flat = [v.reshape(rhs, rows * lanes) for v in (solution, residual, direction_prev, image_prev)]
    turned = residual.transpose(1, 2, 0, 3).reshape(rows, rhs, lanes)
    wide = jnp.concatenate([turned, beside(turned)], axis=0)
    wide = neighbours(wide, "gz", lz)
    upper = neighbours(wide[:, :, : rhs // 2], "gx", lx)
    lower = neighbours(wide[:, :, rhs // 2 :], "gx", lx)
    full = (gathered("gx", lx), gathered("gz", lz))
    ex, ez = lx // 2 + 3, (lz + 14) // 2
    out = jax.ShapeDtypeStruct((rhs, rows * lanes), jnp.float32)
    vmem = pl.BlockSpec(memory_space=pltpu.VMEM)
    smoothed, image, gram = pl.pallas_call(
        functools.partial(smooth_kernel, dims=(lx, lz, rows, lanes), counts=counts, full=full),
        out_shape=(out, out, jax.ShapeDtypeStruct((2 * rhs, 3 * rhs), jnp.float32)),
        in_specs=[pl.BlockSpec(memory_space=pltpu.SMEM)] + [vmem] * 4,
        out_specs=(vmem, vmem, vmem),
        scratch_shapes=[pltpu.VMEM((ex, ez, rhs, 2 * lanes), jnp.float32) for _ in range(4)],
        name="smooth",
    )(where, upper, lower, flat[2], flat[3])
    grams = gather_grams(gram)
    inverse = pl.pallas_call(
        invert_kernel,
        out_shape=jax.ShapeDtypeStruct(gram_prev.shape, jnp.float32),
        in_specs=[vmem],
        out_specs=vmem,
        name="invert",
    )(gram_prev)
    outs = pl.pallas_call(
        finish_kernel,
        out_shape=(jax.ShapeDtypeStruct(residual.shape, jnp.float32),) * 3,
        in_specs=[vmem] * 8,
        out_specs=(vmem,) * 3,
        name="finish",
    )(grams, inverse, *flat, smoothed, image)
    return tuple(outs)


def solution(mesh):
    field = P(None, "gx", "gz", "gy")
    return jax.shard_map(
        body, mesh=mesh, in_specs=(field,) * 4 + (P(),), out_specs=(field,) * 3, check_vma=False
    )
```

```python
import functools

import jax
import jax.numpy as jnp
from jax import lax
from jax.experimental import pallas as pl
from jax.experimental.pallas import tpu as pltpu
from jax.sharding import PartitionSpec as P

HIGHEST = lax.Precision.HIGHEST
REACH = {"gx": (2, 3), "gz": (6, 7), "gy": (14, 15)}
HALO = 16


def shifted(value, axis, step):
    devices = lax.axis_size(axis)
    pairs = [(i, i - step) for i in range(devices) if 0 <= i - step < devices]
    return lax.ppermute(value, axis, pairs)


def block_reach(axis, length):
    low, high = REACH[axis]
    return (-(-low // length), -(-high // length))


def gathered(axis, length):
    low, high = block_reach(axis, length)
    return lax.axis_size(axis) <= low + high + 1


def neighbours(value, axis, length):
    if gathered(axis, length):
        return lax.all_gather(value, axis)
    low, high = block_reach(axis, length)
    return jnp.stack([value if s == 0 else shifted(value, axis, s) for s in range(-low, high + 1)])


def beside(value):
    devices, width = (lax.axis_size("gy"), HALO)
    first, last = value[..., :width], value[..., -width:]
    if devices == 2:
        both = lax.ppermute(jnp.concatenate([first, last], axis=-1), "gy", [(0, 1), (1, 0)])
    else:
        both = jnp.concatenate([shifted(first, "gy", 1), shifted(last, "gy", -1)], axis=-1)
    rows, rhs, lanes = value.shape
    group = lanes // (2 * width)
    both = both.reshape(rows // group, group, rhs, 2, width).transpose(0, 2, 3, 1, 4)
    return both.reshape(rows // group, rhs, lanes)


def smooth_kernel(where, upper, lower, prev, image_prev, smoothed_out, image_out, gram_out, x00, x01, x10, x11, *, dims, counts, full):
    lx, lz, rows, lanes = dims
    nx, nz, ny = counts
    at_x, at_z, at_y = where[0], where[1], where[2]
    total = 2 * lanes
    lane = lax.broadcasted_iota(jnp.int32, (1, total), 1)
    half = lanes // 2
    group = half // HALO
    inside = jnp.ones((1, total), jnp.float32)
    inside = jnp.where((lane >= lanes) & (lane < lanes + half) & (at_y == ny - 1), 0.0, inside)
    inside = jnp.where((lane >= lanes + half) & (at_y == 0), 0.0, inside)
    inside = inside * (1.0 / 26.0)
    even_lanes = jnp.where(lane % 2 == 0, inside, 0.0)
    odd_lanes = jnp.where(lane % 2 == 1, inside, 0.0)
    low_x, low_z = block_low("gx", lx), block_low("gz", lz)

    def source(li, lj):
        gi, gj = at_x * lx + li, at_z * lz + lj
        valid = (gi >= 0) & (gi < nx * lx) & (gj >= 0) & (gj < nz * lz)
        gi, gj = jnp.clip(gi, 0, nx * lx - 1), jnp.clip(gj, 0, nz * lz - 1)
        bx, bz = gi // lx, gj // lz
        sub = (gi - bx * lx) * lz + gj - bz * lz
        bx = bx if full[0] else bx - at_x + low_x
        bz = bz if full[1] else bz - at_z + low_z
        scale = jnp.where(valid, 1.0, 0.0).astype(jnp.float32)
        place = (lj % lz) % group
        main = jnp.concatenate([upper[bx, bz, sub], lower[bx, bz, sub]], axis=0)
        packed = rows + sub // group
        tile = jnp.concatenate([upper[bx, bz, packed], lower[bx, bz, packed]], axis=0)
        after = pltpu.roll(tile, (lanes - HALO * place) % lanes, 1)
        before = pltpu.roll(tile, (half - HALO * (place + 1)) % lanes, 1)
        side = jnp.where(lane[:, :lanes] < half, after, before)
        return jnp.concatenate([main, side], axis=1), even_lanes * scale, odd_lanes * scale

    def pair(x):
        return pltpu.roll(x, 1, 1) + pltpu.roll(x, total - 1, 1)

    def box(x):
        return x + pair(x)

    ex, ez = lx // 2 + 3, (lz + 14) // 2

    def sides_j0(ref, a, b):
        return ref[a, b - 1] + ref[a, b]

    def sides_j1(ref, a, b):
        return ref[a, b] + ref[a, b + 1]

    def loop(count, start, step):
        def run(a, carry):
            step(a)
            return carry

        lax.fori_loop(start, start + count, run, 0)

    def f0e(a):
        for b in range(ez):
            r, se, so = source(-2 + 2 * a, -6 + 2 * b)
            xe = r * se
            x00[a, b] = xe + (r + pair(xe)) * so

    def f0o(a):
        for b in range(ez - 1):
            r, se, so = source(-2 + 2 * a, -5 + 2 * b)
            q = r + box(sides_j1(x00, a, b))
            xe = q * se
            x01[a, b] = xe + (q + pair(xe)) * so

    def f1e(a):
        for b in range(1, ez - 1):
            r, se, so = source(-1 + 2 * a, -6 + 2 * b)
            near = x00[a, b] + x00[a + 1, b] + sides_j0(x01, a, b) + sides_j0(x01, a + 1, b)
            q = r + box(near)
            xe = q * se
            x10[a, b] = xe + (q + pair(xe)) * so

    def f1o(a):
        for b in range(1, ez - 2):
            r, se, so = source(-1 + 2 * a, -5 + 2 * b)
            near = x01[a, b] + x01[a + 1, b] + sides_j1(x00, a, b) + sides_j1(x00, a + 1, b) + sides_j1(x10, a, b)
            q = r + box(near)
            xo = (q + pair(q * se)) * so
            x11[a, b] = (q + pair(xo)) * se + xo

    def b1e(a):
        for b in range(2, ez - 2):
            r, se, so = source(-1 + 2 * a, -6 + 2 * b)
            near = x00[a, b] + x00[a + 1, b] + sides_j0(x01, a, b) + sides_j0(x01, a + 1, b) + sides_j0(x11, a, b)
            q = r + box(near)
            xo = (q + pair(x10[a, b])) * so
            x10[a, b] = (q + pair(xo)) * se + xo

    def b0o(a):
        for b in range(2, ez - 3):
            r, se, so = source(-2 + 2 * a, -5 + 2 * b)
            near = x11[a - 1, b] + x11[a, b] + sides_j1(x10, a - 1, b) + sides_j1(x10, a, b) + sides_j1(x00, a, b)
            q = r + box(near)
            xo = (q + pair(x01[a, b])) * so
            x01[a, b] = (q + pair(xo)) * se + xo

    def b0e(a):
        for b in range(3, ez - 3):
            r, se, so = source(-2 + 2 * a, -6 + 2 * b)
            near = x10[a - 1, b] + x10[a, b] + sides_j0(x11, a - 1, b) + sides_j0(x11, a, b) + sides_j0(x01, a, b)
            q = r + box(near)
            xo = (q + pair(x00[a, b])) * so
            x00[a, b] = (q + pair(xo)) * se + xo

    loop(ex, 0, f0e)
    loop(ex, 0, f0o)
    loop(ex - 1, 0, f1e)
    loop(ex - 1, 0, f1o)
    loop(ex - 1, 0, b1e)
    loop(ex - 2, 1, b0o)
    loop(ex - 2, 1, b0e)

    def cell(i, j):
        a = (i + 2) // 2 if i % 2 == 0 else (i + 1) // 2
        b = (j + 6) // 2 if j % 2 == 0 else (j + 5) // 2
        return ((x00, x01), (x10, x11))[i % 2][j % 2][a, b]

    own = []
    for i in range(lx):
        for j in range(lz):
            near = functools.reduce(jnp.add, [cell(i + u, j + v) for u in (-1, 0, 1) for v in (-1, 0, 1)])
            mine = cell(i, j)
            image = 27.0 * mine - box(near)
            at = (i * lz + j) * lanes
            smoothed_out[:, at : at + lanes] = mine[:, :lanes]
            image_out[:, at : at + lanes] = image[:, :lanes]
            own.append(source(i, j)[0][:, :lanes])
    left = jnp.concatenate([smoothed_out[...], prev[...]], axis=0)
    right = jnp.concatenate([jnp.concatenate(own, axis=1), image_out[...], image_prev[...]], axis=0)
    gram_out[...] = lax.dot_general(left, right, (((1,), (1,)), ((), ())), precision=HIGHEST)


def block_low(axis, length):
    return -(-REACH[axis][0] // length)


def spd_solve(matrix, target):
    order = matrix.shape[0]
    sym = 0.5 * (matrix + matrix.T)
    work = jnp.concatenate([sym, target], axis=1)
    row = lax.broadcasted_iota(jnp.int32, (order, 1), 0)
    for k in range(order):
        scaled = work[k : k + 1] / work[k : k + 1, k : k + 1]
        factor = work[:, k : k + 1]
        work = jnp.where(row == k, scaled, work - factor * scaled)
    return work[:, order:]


def dot(left, right):
    return jnp.dot(left, right, precision=HIGHEST)


def flattened(ref):
    _, lx, lz, _ = ref.shape
    return jnp.concatenate([ref[:, i, j, :] for i in range(lx) for j in range(lz)], axis=1)


def invert_kernel(matrix, out):
    order = matrix.shape[0]
    row = lax.broadcasted_iota(jnp.int32, (order, order), 0)
    col = lax.broadcasted_iota(jnp.int32, (order, order), 1)
    out[...] = spd_solve(matrix[...], jnp.where(row == col, 1.0, 0.0).astype(jnp.float32))


def finish_kernel(grams, inverse, solution, residual, prev, image_prev, smoothed, image, solution_out, residual_out, direction_out):
    n = inverse.shape[0]
    total = jnp.sum(grams[...], axis=0)
    gram_zr, gram_zw, gram_zq = total[:n, :n], total[:n, n : 2 * n], total[:n, 2 * n :]
    gram_pw, gram_pq = total[n:, n : 2 * n], total[n:, 2 * n :]
    beta = dot(inverse[...], gram_zr)
    turned = beta.T
    curvature = gram_zw + dot(gram_zq, beta) + dot(turned, gram_pw + dot(gram_pq, beta))
    direction = smoothed[...] + dot(turned, prev[...])
    image_new = image[...] + dot(turned, image_prev[...])
    alpha = spd_solve(curvature, gram_zr).T
    values = (direction, flattened(solution) + dot(alpha, direction), flattened(residual) - dot(alpha, image_new))
    _, lx, lz, lanes = direction_out.shape
    for value, out in zip(values, (direction_out, solution_out, residual_out)):
        for i in range(lx):
            for j in range(lz):
                at = (i * lz + j) * lanes
                out[:, i, j, :] = value[:, at : at + lanes]


def gather_grams(gram):
    for axis in ("gx", "gy", "gz"):
        others = [lax.ppermute(gram, axis, [(i, (i + k) % lax.axis_size(axis)) for i in range(lax.axis_size(axis))])
                  for k in range(1, lax.axis_size(axis))]
        gram = functools.reduce(jnp.add, others, gram)
    return gram[None]


def body(solution, residual, direction_prev, image_prev, gram_prev):
    rhs, lx, lz, lanes = residual.shape
    rows = lx * lz
    counts = tuple(lax.axis_size(axis) for axis in ("gx", "gz", "gy"))
    where = jnp.stack([lax.axis_index(axis) for axis in ("gx", "gz", "gy")]).astype(jnp.int32)
    flat = [v.reshape(rhs, rows * lanes) for v in (solution, residual, direction_prev, image_prev)]
    turned = residual.transpose(1, 2, 0, 3).reshape(rows, rhs, lanes)
    wide = jnp.concatenate([turned, beside(turned)], axis=0)
    wide = neighbours(wide, "gz", lz)
    upper = neighbours(wide[:, :, : rhs // 2], "gx", lx)
    lower = neighbours(wide[:, :, rhs // 2 :], "gx", lx)
    full = (gathered("gx", lx), gathered("gz", lz))
    ex, ez = lx // 2 + 3, (lz + 14) // 2
    out = jax.ShapeDtypeStruct((rhs, rows * lanes), jnp.float32)
    vmem = pl.BlockSpec(memory_space=pltpu.VMEM)
    smoothed, image, gram = pl.pallas_call(
        functools.partial(smooth_kernel, dims=(lx, lz, rows, lanes), counts=counts, full=full),
        out_shape=(out, out, jax.ShapeDtypeStruct((2 * rhs, 3 * rhs), jnp.float32)),
        in_specs=[pl.BlockSpec(memory_space=pltpu.SMEM)] + [vmem] * 4,
        out_specs=(vmem, vmem, vmem),
        scratch_shapes=[pltpu.VMEM((ex, ez, rhs, 2 * lanes), jnp.float32) for _ in range(4)],
        name="smooth",
    )(where, upper, lower, flat[2], flat[3])
    grams = gather_grams(gram)
    inverse = pl.pallas_call(
        invert_kernel,
        out_shape=jax.ShapeDtypeStruct(gram_prev.shape, jnp.float32),
        in_specs=[vmem],
        out_specs=vmem,
        name="invert",
    )(gram_prev)
    outs = pl.pallas_call(
        finish_kernel,
        out_shape=(jax.ShapeDtypeStruct(residual.shape, jnp.float32),) * 3,
        in_specs=[vmem] * 8,
        out_specs=(vmem,) * 3,
        name="finish",
    )(grams, inverse, solution, residual, flat[2], flat[3], smoothed, image)
    return tuple(outs)


def solution(mesh):
    field = P(None, "gx", "gz", "gy")
    return jax.shard_map(
        body, mesh=mesh, in_specs=(field,) * 4 + (P(),), out_specs=(field,) * 3, check_vma=False
    )
```
